32 devices in a mesh: dp: 8 (over z, y), tensor: 4 (over x, core).
Axes of the slice: x: 2, y: 2, z: 4, core: 2. Of those that a mesh axis runs over, the one named last changes fastest.
Arguments:
- tokens: bfloat16 [2048, 768], P('dp'), may hold values from -6 to 6
- cotangent: bfloat16 [2048, 768], P('dp'), may hold values from -6 to 6
- norm_gain: float32 [2, 768], replicated, may hold values from 0.5 to 1.5
- w_z: bfloat16 [2, 768, 1536], P(None, None, 'tensor'), may hold values from -0.21875 to 0.21875
- w_x: bfloat16 [2, 768, 1536], P(None, None, 'tensor'), may hold values from -0.21875 to 0.21875
- w_bc: bfloat16 [2, 768, 256], replicated, may hold values from -0.21875 to 0.21875
- w_dt: bfloat16 [2, 768, 24], P(None, None, 'tensor'), may hold values from -0.21875 to 0.21875
- conv_x: float32 [2, 4, 1536], P(None, None, 'tensor'), may hold values from -3 to 3
- conv_x_bias: float32 [2, 1536], P(None, 'tensor'), may hold values from -3 to 3
- conv_bc: float32 [2, 4, 256], replicated, may hold values from -3 to 3
- conv_bc_bias: float32 [2, 256], replicated, may hold values from -3 to 3
- dt_bias: float32 [2, 24], P(None, 'tensor'), may hold values from -6 to -2
- a_log: float32 [2, 24], P(None, 'tensor'), may hold values from 0 to 2.77
- d_skip: float32 [2, 24], P(None, 'tensor'), may hold values from 0.5 to 1.5
- gate_gain: float32 [2, 1536], P(None, 'tensor'), may hold values from 0.5 to 1.5
- w_out: bfloat16 [2, 1536, 768], P(None, 'tensor'), may hold values from -0.15625 to 0.15625
Outputs:
- output: float32 [2048, 768], P('dp')
- input_grad: float32 [2048, 768], P('dp')
- grad_norm_gain: float32 [2, 768], P(None, 'dp')
- grad_w_z: float32 [2, 768, 1536], P(None, 'dp', 'tensor')
- grad_w_x: float32 [2, 768, 1536], P(None, 'dp', 'tensor')
- grad_w_dt: float32 [2, 768, 24], P(None, 'dp', 'tensor')
- grad_w_out: float32 [2, 1536, 768], P(None, 'tensor', 'dp')
- grad_channels: float32 [2, 6, 24, 64], P(None, None, 'tensor', 'dp')
- grad_w_bc: float32 [2, 768, 256], P(None, ('dp', 'tensor'))
- grad_bc_conv: float32 [2, 5, 256], P(None, None, ('dp', 'tensor'))
- grad_heads: float32 [2, 3, 24], P(None, None, 'tensor')
The draws below stay inside these ranges and needn't reach their ends.
All inputs are finite; a program needn't handle non-finite values.
Results may differ from the reference program's by a relative error of at most 0.012.
Values sent between devices are 32-bit elements; how exact they have to be, the bound alone decides.
A program may use at most 128 MiB of HBM per device.

```python
import jax
import jax.numpy as jnp
from jax import lax

D = 768
INNER = 1536
HEADS = 24
P_SIZE = 64
N = 128
K = 4
GROUP = 128
LENGTH = 256
LAYERS = 2
SEQS = 8
TOKENS = 2048


def with_spikes(array, rng, source, target, blocks, factor):
    def block_of(position):
        return (jnp.arange(array.shape[position]) // (array.shape[position] // blocks)).reshape((-1,) + (1,) * (array.ndim - 1 - position))

    one_side = jax.random.permutation(rng, blocks)[block_of(target)]
    far = (block_of(target) + blocks // 2) % blocks
    return jnp.where((block_of(source) == one_side) | (block_of(source) == far), factor * array, array)


def level_of(stream_key, shape, cuts, least, high):
    level = 1.0
    for axis_at, parts in cuts:
        draws = jax.random.uniform(jax.random.fold_in(jax.random.fold_in(stream_key, 6), axis_at), (parts,), jnp.float32, least / len(cuts), high / len(cuts))
        level = level * jnp.repeat(jnp.exp(draws), shape[axis_at] // parts).reshape((-1,) + (1,) * (len(shape) - 1 - axis_at))
    return level


def noise(rng, dims, scale, most, shards=(), held_as=jnp.bfloat16):
    array = scale * jax.random.normal(rng, dims, jnp.float32)
    if shards:
        array = array * level_of(rng, dims, shards, -0.22, 0.18)
    return jnp.clip(array, -most, most).astype(held_as)


def noise_with(own_key, shape, scale, reach, pieces, heavy, kind=jnp.bfloat16):
    values = scale * jax.random.normal(own_key, shape, jnp.float32)
    if pieces:
        values = values * level_of(own_key, shape, pieces, -0.22, 0.18)
    return jnp.clip(with_spikes(values, jax.random.fold_in(own_key, 3), *heavy), -reach, reach).astype(kind)


def setup_inputs(seed: int = 0) -> dict:
    key_list = jax.random.split(jax.random.key(seed), 17)
    return {
        "tokens": noise_with(key_list[0], (TOKENS, D), 1.0, 6.0, ((0, 8),), (0, 1, 8, 2.0)),
        "cotangent": noise_with(key_list[1], (TOKENS, D), 1.0, 6.0, ((0, 8),), (0, 1, 8, 2.0)),
        "norm_gain": jnp.clip(1.0 + 0.1 * jax.random.normal(key_list[2], (LAYERS, D), jnp.float32), 0.5, 1.5),
        "w_z": noise(key_list[3], (LAYERS, D, INNER), D ** -0.5, 0.21875, ((2, 4),)),
        "w_x": noise(key_list[4], (LAYERS, D, INNER), D ** -0.5, 0.21875, ((2, 4),)),
        "w_bc": noise(key_list[5], (LAYERS, D, 2 * N), D ** -0.5, 0.21875),
        "w_dt": noise(key_list[6], (LAYERS, D, HEADS), D ** -0.5, 0.21875, ((2, 4),)),
        "conv_x": noise(key_list[7], (LAYERS, K, INNER), K ** -0.5, 3.0, ((2, 4),), jnp.float32),
        "conv_x_bias": noise(key_list[8], (LAYERS, INNER), 0.5, 3.0, ((1, 4),), jnp.float32),
        "conv_bc": noise(key_list[9], (LAYERS, K, 2 * N), K ** -0.5, 3.0, (), jnp.float32),
        "conv_bc_bias": noise(key_list[10], (LAYERS, 2 * N), 0.5, 3.0, (), jnp.float32),
        "dt_bias": jnp.clip(-6.0 + 4.0 * jax.random.uniform(key_list[11], (LAYERS, HEADS), jnp.float32) ** level_of(key_list[11], (LAYERS, HEADS), ((1, 4),), -0.2, 0.2), -6.0, -2.0),
        "a_log": jnp.clip(2.77 * jax.random.uniform(key_list[12], (LAYERS, HEADS), jnp.float32) ** level_of(key_list[12], (LAYERS, HEADS), ((1, 4),), -0.2, 0.2), 0.0, 2.77),
        "d_skip": jnp.clip(0.5 + 1.0 * jax.random.uniform(key_list[13], (LAYERS, HEADS), jnp.float32) ** level_of(key_list[13], (LAYERS, HEADS), ((1, 4),), -0.2, 0.2), 0.5, 1.5),
        "gate_gain": jnp.clip(1.0 + 0.1 * jax.random.normal(key_list[14], (LAYERS, INNER), jnp.float32), 0.5, 1.5),
        "w_out": noise(key_list[15], (LAYERS, INNER, D), INNER ** -0.5, 0.15625, ((1, 4),)),
    }


EPSILON = 1e-05
HIGHEST_PREC = lax.Precision.HIGHEST

def project(left, right):
    return jnp.dot(left, right, preferred_element_type=jnp.float32)

def causal_conv(signal, kernel, offset_vec):
    tap_count = kernel.shape[0]
    row_count = signal.shape[0]
    padded = jnp.pad(signal, ((tap_count - 1, 0), (0, 0)))
    running = jnp.zeros_like(signal) + offset_vec[None, :]
    for tap_index in range(tap_count):
        running = running + kernel[tap_index][None, :] * padded[tap_index:tap_index + row_count]
    return running

def mixer_core(inner_in, state_in, step_in, gate_in, kernel_x, shift_x, kernel_bc, shift_bc, step_bias, decay_log, skip_coef):
    length = inner_in.shape[0]
    head_count = step_in.shape[1]
    head_width = inner_in.shape[1] // head_count
    state_size = state_in.shape[1] // 2
    blocks = length // GROUP
    inner_conv = jax.nn.silu(causal_conv(inner_in, kernel_x, shift_x))
    state_conv = jax.nn.silu(causal_conv(state_in, kernel_bc, shift_bc))
    key_cols = state_conv[:, :state_size].reshape(blocks, GROUP, state_size)
    query_cols = state_conv[:, state_size:].reshape(blocks, GROUP, state_size)
    step_size = jax.nn.softplus(step_in + step_bias[None, :])
    log_rate = (step_size * (-jnp.exp(decay_log))[None, :]).reshape(blocks, GROUP, head_count)
    step_size = step_size.reshape(blocks, GROUP, head_count)
    values = inner_conv.reshape(blocks, GROUP, head_count, head_width)
    log_decay = jnp.cumsum(log_rate, axis=1)
    causal = jnp.tril(jnp.ones((GROUP, GROUP), dtype=bool))[None, :, :, None]
    log_gap = log_decay[:, :, None, :] - log_decay[:, None, :, :]
    decay_mask = jnp.where(causal, jnp.exp(jnp.where(causal, log_gap, 0.0)), 0.0)
    scores = jnp.einsum('qin,qjn->qij', query_cols, key_cols, precision=HIGHEST_PREC)
    weighted = values * step_size[..., None]
    block_weights = scores[..., None] * decay_mask
    within = jnp.einsum('qijh,qjhp->qihp', block_weights, weighted, precision=HIGHEST_PREC)
    to_end = jnp.exp(log_decay[:, -1:, :] - log_decay)
    states = jnp.einsum('qjn,qjhp->qhnp', key_cols, weighted * to_end[..., None], precision=HIGHEST_PREC)
    block_decay = jnp.exp(log_decay[:, -1, :])

    def carry_block(carried, inputs_pair):
        block_state, block_factor = inputs_pair
        return (carried * block_factor[:, None, None] + block_state, carried)
    initial = jnp.zeros((head_count, state_size, head_width), inner_in.dtype)
    _, before = lax.scan(carry_block, initial, (states, block_decay))
    across = jnp.einsum('qin,qhnp->qihp', query_cols, before, precision=HIGHEST_PREC) * jnp.exp(log_decay)[..., None]
    mixed = within + across + values * skip_coef[None, None, :, None]
    return mixed.reshape(length, head_count * head_width) * jax.nn.silu(gate_in)

def layer_forward(residual, params):
    norm_vec, wz_mat, wx_mat, wbc_mat, wdt_mat, kernel_x, shift_x, kernel_bc, shift_bc, step_bias, decay_log, skip_coef, gate_vec, wout_mat = params
    rescale = lax.rsqrt(lax.optimization_barrier(jnp.mean(residual * residual, axis=1, keepdims=True)) + EPSILON)
    normed = (residual * rescale * norm_vec[None, :]).astype(jnp.bfloat16)
    core_out = mixer_core(project(normed, wx_mat), project(normed, wbc_mat), project(normed, wdt_mat), project(normed, wz_mat), kernel_x, shift_x, kernel_bc, shift_bc, step_bias, decay_log, skip_coef)
    square = lax.optimization_barrier(jnp.mean(core_out * core_out, axis=1, keepdims=True))
    gated_out = (core_out * gate_vec[None, :]).astype(jnp.bfloat16)
    branch = project(gated_out, wout_mat)
    return residual + lax.rsqrt(square + EPSILON) * branch

def layer_backward(residual, params, upstream):
    norm_vec, wz_mat, wx_mat, wbc_mat, wdt_mat, kernel_x, shift_x, kernel_bc, shift_bc, step_bias, decay_log, skip_coef, gate_vec, wout_mat = params
    rescale = lax.rsqrt(lax.optimization_barrier(jnp.mean(residual * residual, axis=1, keepdims=True)) + EPSILON)
    normed = (residual * rescale * norm_vec[None, :]).astype(jnp.bfloat16)
    core_out, pull = jax.vjp(mixer_core, project(normed, wx_mat), project(normed, wbc_mat), project(normed, wdt_mat), project(normed, wz_mat), kernel_x, shift_x, kernel_bc, shift_bc, step_bias, decay_log, skip_coef)
    square = lax.optimization_barrier(jnp.mean(core_out * core_out, axis=1, keepdims=True))
    factor = lax.rsqrt(square + EPSILON)
    gated_out = (core_out * gate_vec[None, :]).astype(jnp.bfloat16)
    branch = project(gated_out, wout_mat)
    back_branch = (upstream * factor).astype(jnp.bfloat16)
    grad_wout = project(gated_out.T, back_branch)
    back_factor = lax.optimization_barrier(jnp.sum(upstream * branch, axis=1, keepdims=True))
    back_square = -0.5 * back_factor * factor * factor * factor
    back_gated = project(back_branch, wout_mat.T)
    grad_gate = lax.optimization_barrier(jnp.sum(back_gated * core_out, axis=0))
    back_core = back_gated * gate_vec[None, :] + back_square * 2.0 * core_out / INNER
    back_inner, back_state, back_step, back_gate, grad_kx, grad_sx, grad_kbc, grad_sbc, grad_bias, grad_decay, grad_skip = pull(back_core)
    back_inner = back_inner.astype(jnp.bfloat16)
    back_state = back_state.astype(jnp.bfloat16)
    back_step = back_step.astype(jnp.bfloat16)
    back_gate = back_gate.astype(jnp.bfloat16)
    grad_wz = project(normed.T, back_gate)
    grad_wx = project(normed.T, back_inner)
    grad_wbc = project(normed.T, back_state)
    grad_wdt = project(normed.T, back_step)
    back_normed = project(back_gate, wz_mat.T) + project(back_inner, wx_mat.T) + project(back_state, wbc_mat.T) + project(back_step, wdt_mat.T)
    grad_norm = lax.optimization_barrier(jnp.sum(back_normed * residual * rescale, axis=0))
    back_hat = back_normed * norm_vec[None, :]
    back_resid = upstream + rescale * back_hat - rescale * rescale * rescale * residual * lax.optimization_barrier(jnp.mean(back_hat * residual, axis=1, keepdims=True))
    grad_chan = jnp.concatenate([grad_kx, grad_sx[None, :], grad_gate[None, :]], axis=0)
    grad_bcconv = jnp.concatenate([grad_kbc, grad_sbc[None, :]], axis=0)
    grad_heads = jnp.stack([grad_decay, grad_skip, grad_bias])
    return (back_resid, (grad_norm, grad_wz, grad_wx, grad_wdt, grad_wout, grad_chan, grad_wbc, grad_bcconv, grad_heads))

def reference(tokens, cotangent, norm_gain, w_z, w_x, w_bc, w_dt, conv_x, conv_x_bias, conv_bc, conv_bc_bias, dt_bias, a_log, d_skip, gate_gain, w_out):
    all_params = (norm_gain, w_z, w_x, w_bc, w_dt, conv_x, conv_x_bias, conv_bc, conv_bc_bias, dt_bias, a_log, d_skip, gate_gain, w_out)

    def take_layer(layer_index):
        return tuple((param[layer_index] for param in all_params))
    zero_grads = (jnp.zeros((LAYERS, D), jnp.float32), jnp.zeros((LAYERS, D, INNER), jnp.float32), jnp.zeros((LAYERS, D, INNER), jnp.float32), jnp.zeros((LAYERS, D, HEADS), jnp.float32), jnp.zeros((LAYERS, INNER, D), jnp.float32), jnp.zeros((LAYERS, K + 2, INNER), jnp.float32), jnp.zeros((LAYERS, D, 2 * N), jnp.float32), jnp.zeros((LAYERS, K + 1, 2 * N), jnp.float32), jnp.zeros((LAYERS, 3, HEADS), jnp.float32))

    def one_sequence(totals, inputs_pair):
        seq_tokens, seq_cot = inputs_pair
        residual = seq_tokens.astype(jnp.float32)
        layer_inputs = []
        for layer_index in range(LAYERS):
            layer_inputs.append(residual)
            residual = layer_forward(residual, take_layer(layer_index))
        upstream = seq_cot.astype(jnp.float32)
        per_layer = [None] * LAYERS
        for layer_index in reversed(range(LAYERS)):
            upstream, per_layer[layer_index] = layer_backward(layer_inputs[layer_index], take_layer(layer_index), upstream)
        stacked = tuple((jnp.stack([per_layer[which][item] for which in range(LAYERS)]) for item in range(9)))
        totals = tuple((running + extra for running, extra in zip(totals, stacked)))
        return (totals, (residual, upstream))
    totals, (outputs, grads_in) = lax.scan(one_sequence, zero_grads, (tokens.reshape(SEQS, LENGTH, D), cotangent.reshape(SEQS, LENGTH, D)))
    return (outputs.reshape(TOKENS, D), grads_in.reshape(TOKENS, D), totals[0], totals[1], totals[2], totals[3], totals[4], totals[5].reshape(LAYERS, K + 2, HEADS, P_SIZE), totals[6], totals[7], totals[8])
```

```python
import functools

import jax
import jax.numpy as jnp
from jax import lax
from jax.sharding import PartitionSpec as P

INNER = 1536
P_SIZE = 64
K = 4
GROUP = 128
LENGTH = 256
LAYERS = 2


EPSILON = 1e-05
HIGHEST_PREC = lax.Precision.HIGHEST


def project(left, right):
    return jnp.dot(left, right, preferred_element_type=jnp.float32)


def weight_grad(left, right):
    return jnp.einsum("rd,rc->dc", left, right, preferred_element_type=jnp.float32)


def input_back(left, right):
    return jnp.einsum("rc,dc->rd", left, right, preferred_element_type=jnp.float32)


def exchange(value, axis, size, bit):
    step = 1 << bit
    return lax.ppermute(value, axis, [(i, i ^ step) for i in range(size)])


def bit_of(axis, bit):
    return (lax.axis_index(axis) >> bit) & 1


def halve(value, axis, size, bit, dim):
    mine = bit_of(axis, bit)
    keep = lax.dynamic_index_in_dim(value, mine, dim, keepdims=False)
    send = lax.dynamic_index_in_dim(value, 1 - mine, dim, keepdims=False)
    return keep + exchange(send, axis, size, bit)


def scatter_sum(value, axis, size, dim):
    left = size
    bit = 0
    while left > 1:
        left //= 2
        shape = value.shape
        value = value.reshape(shape[:dim] + (left, 2) + shape[dim + 1 :])
        value = halve(value, axis, size, bit, dim + 1)
        bit += 1
    return lax.squeeze(value, (dim,))


def full_sum(value, axis, size, first=0):
    bit = first
    while (1 << bit) < size:
        value = value + exchange(value, axis, size, bit)
        bit += 1
    return value


def row_sum(value, axis, size, chunks=2):
    rows, width = value.shape
    mine = bit_of(axis, 0)
    parts = value.reshape(chunks, 2, rows // (2 * chunks), width)
    done = []
    for index in range(chunks):
        half = halve(parts[index], axis, size, 0, 0)
        half = full_sum(half, axis, size, 1)
        other = exchange(half, axis, size, 0)
        low = jnp.where(mine == 0, half, other)
        high = jnp.where(mine == 0, other, half)
        done += [low, high]
    return jnp.concatenate(done, axis=0)


def causal_conv(signal, kernel, offset_vec):
    tap_count = kernel.shape[0]
    row_count = signal.shape[0]
    padded = jnp.pad(signal, ((tap_count - 1, 0), (0, 0)))
    running = jnp.zeros_like(signal) + offset_vec[None, :]
    for tap_index in range(tap_count):
        running = running + kernel[tap_index][None, :] * padded[tap_index : tap_index + row_count]
    return running


def mixer_core(
    inner_in,
    state_in,
    step_in,
    gate_in,
    kernel_x,
    shift_x,
    kernel_bc,
    shift_bc,
    step_bias,
    decay_log,
    skip_coef,
):
    length = inner_in.shape[0]
    head_count = step_in.shape[1]
    head_width = inner_in.shape[1] // head_count
    state_size = state_in.shape[1] // 2
    blocks = length // GROUP
    inner_conv = jax.nn.silu(causal_conv(inner_in, kernel_x, shift_x))
    state_conv = jax.nn.silu(causal_conv(state_in, kernel_bc, shift_bc))
    key_cols = state_conv[:, :state_size].reshape(blocks, GROUP, state_size)
    query_cols = state_conv[:, state_size:].reshape(blocks, GROUP, state_size)
    step_size = jax.nn.softplus(step_in + step_bias[None, :])
    log_rate = (step_size * (-jnp.exp(decay_log))[None, :]).reshape(blocks, GROUP, head_count)
    step_size = step_size.reshape(blocks, GROUP, head_count)
    values = inner_conv.reshape(blocks, GROUP, head_count, head_width)
    log_decay = jnp.cumsum(log_rate, axis=1)
    causal = jnp.tril(jnp.ones((GROUP, GROUP), dtype=bool))[None, :, :, None]
    log_gap = log_decay[:, :, None, :] - log_decay[:, None, :, :]
    decay_mask = jnp.where(causal, jnp.exp(jnp.where(causal, log_gap, 0.0)), 0.0)
    scores = jnp.einsum("qin,qjn->qij", query_cols, key_cols, precision=HIGHEST_PREC)
    weighted = values * step_size[..., None]
    block_weights = scores[..., None] * decay_mask
    within = jnp.einsum("qijh,qjhp->qihp", block_weights, weighted, precision=HIGHEST_PREC)
    to_end = jnp.exp(log_decay[:, -1:, :] - log_decay)
    states = jnp.einsum(
        "qjn,qjhp->qhnp", key_cols, weighted * to_end[..., None], precision=HIGHEST_PREC
    )
    block_decay = jnp.exp(log_decay[:, -1, :])

    def carry_block(carried, inputs_pair):
        block_state, block_factor = inputs_pair
        return (carried * block_factor[:, None, None] + block_state, carried)

    initial = jnp.zeros((head_count, state_size, head_width), inner_in.dtype)
    _, before = lax.scan(carry_block, initial, (states, block_decay))
    across = (
        jnp.einsum("qin,qhnp->qihp", query_cols, before, precision=HIGHEST_PREC)
        * jnp.exp(log_decay)[..., None]
    )
    mixed = within + across + values * skip_coef[None, None, :, None]
    return mixed.reshape(length, head_count * head_width) * jax.nn.silu(gate_in)


def batched_core(seq_count):

    def apply_core(
        inner_in,
        state_in,
        step_in,
        gate_in,
        kernel_x,
        shift_x,
        kernel_bc,
        shift_bc,
        step_bias,
        decay_log,
        skip_coef,
    ):
        mapped = jax.vmap(
            mixer_core, in_axes=(0, 0, 0, 0, None, None, None, None, None, None, None)
        )(
            inner_in.reshape(seq_count, -1, inner_in.shape[1]),
            state_in.reshape(seq_count, -1, state_in.shape[1]),
            step_in.reshape(seq_count, -1, step_in.shape[1]),
            gate_in.reshape(seq_count, -1, gate_in.shape[1]),
            kernel_x,
            shift_x,
            kernel_bc,
            shift_bc,
            step_bias,
            decay_log,
            skip_coef,
        )
        return mapped.reshape(inner_in.shape)

    return apply_core


def reduce_grads(dp_size, tensor_size, g_norm, g_wz, g_wx, g_wdt, g_wout, g_chan, g_wbc, g_bcc, g_heads):
    width = g_norm.shape[0]
    own = width // dp_size
    heads = g_wdt.shape[1]
    channels = g_wz.shape[1]
    taps = g_chan.shape[0]
    lanes = P_SIZE // dp_size

    def blocks(grad):
        return grad.reshape(dp_size, own, channels)

    out_t = scatter_sum(blocks(g_wout), "dp", dp_size, 0)
    r_wx = scatter_sum(blocks(g_wx), "dp", dp_size, 0)
    r_wz = scatter_sum(blocks(g_wz), "dp", dp_size, 0)
    chan = g_chan.reshape(taps, heads, dp_size, lanes).transpose(2, 0, 1, 3)
    small = jnp.concatenate(
        [
            g_wdt.reshape(dp_size, own * heads),
            g_norm.reshape(dp_size, own),
            chan.reshape(dp_size, taps * heads * lanes),
            jnp.broadcast_to(g_heads.reshape(1, 3 * heads), (dp_size, 3 * heads)),
        ],
        axis=1,
    )
    used = small.shape[1]
    padded = -(-used // 1024) * 1024
    small = jnp.pad(small, ((0, 0), (0, padded - used))).reshape(dp_size, padded // 128, 128)
    small = scatter_sum(small, "dp", dp_size, 0).reshape(padded)
    at = [own * heads, own, taps * heads * lanes, 3 * heads]
    r_wdt = small[: at[0]].reshape(own, heads)
    r_norm = small[at[0] : at[0] + at[1]]
    r_chan = small[at[0] + at[1] : sum(at[:3])].reshape(taps, heads, lanes)
    r_heads = small[sum(at[:3]) : used].reshape(3, heads)
    both = g_wbc.shape[1]
    cut = width // (dp_size * tensor_size)
    piece = both // (dp_size * tensor_size)
    rows = g_bcc.shape[0]
    conv = g_bcc.reshape(rows, dp_size, tensor_size, piece).transpose(1, 2, 0, 3)
    conv = conv.reshape(dp_size, tensor_size, 1, rows * piece)
    conv = jnp.pad(conv, ((0, 0), (0, 0), (0, 0), (0, both - rows * piece)))
    shared = jnp.concatenate([g_wbc.reshape(dp_size, tensor_size, cut, both), conv], axis=2)
    shared = scatter_sum(shared, "tensor", tensor_size, 1)
    shared = scatter_sum(shared, "dp", dp_size, 0)
    r_wbc = shared[:cut]
    r_bcc = shared[cut, : rows * piece].reshape(rows, piece)
    return (r_norm, r_wz, r_wx, r_wdt, out_t.T, r_chan, r_wbc, r_bcc, r_heads)


def on_device(
    dp_size,
    tensor_size,
    tokens,
    cotangent,
    norm_gain,
    w_z,
    w_x,
    w_bc,
    w_dt,
    conv_x,
    conv_x_bias,
    conv_bc,
    conv_bc_bias,
    dt_bias,
    a_log,
    d_skip,
    gate_gain,
    w_out,
):
    seq_count = tokens.shape[0] // LENGTH
    core_fn = batched_core(seq_count)
    residual = tokens.astype(jnp.float32)
    saved = []
    for layer_index in range(LAYERS):
        rescale = lax.rsqrt(jnp.mean(residual * residual, axis=1, keepdims=True) + EPSILON)
        normed = (residual * rescale * norm_gain[layer_index][None, :]).astype(jnp.bfloat16)
        gate_in = project(normed, w_z[layer_index])
        inner_in = project(normed, w_x[layer_index])
        state_in = project(normed, w_bc[layer_index])
        step_in = project(normed, w_dt[layer_index])
        core_out = core_fn(
            inner_in,
            state_in,
            step_in,
            gate_in,
            conv_x[layer_index],
            conv_x_bias[layer_index],
            conv_bc[layer_index],
            conv_bc_bias[layer_index],
            dt_bias[layer_index],
            a_log[layer_index],
            d_skip[layer_index],
        )
        local_square = jnp.sum(core_out * core_out, axis=1, keepdims=True)
        gated_out = (core_out * gate_gain[layer_index][None, :]).astype(jnp.bfloat16)
        partial_value = project(gated_out, w_out[layer_index])
        rows = local_square.shape[0]
        total_square = full_sum(local_square.reshape(rows // 128, 128), "tensor", tensor_size)
        factor = lax.rsqrt(total_square.reshape(rows, 1) / INNER + EPSILON)
        update = row_sum(partial_value, "tensor", tensor_size)
        saved.append(
            (residual, rescale, normed, inner_in, state_in, step_in, gate_in, factor, update)
        )
        residual = residual + factor * update
    output = residual
    upstream = cotangent.astype(jnp.float32)
    owned = []
    for layer_index in reversed(range(LAYERS)):
        residual, rescale, normed, inner_in, state_in, step_in, gate_in, factor, update = saved[
            layer_index
        ]
        core_out, pull = jax.vjp(
            core_fn,
            inner_in,
            state_in,
            step_in,
            gate_in,
            conv_x[layer_index],
            conv_x_bias[layer_index],
            conv_bc[layer_index],
            conv_bc_bias[layer_index],
            dt_bias[layer_index],
            a_log[layer_index],
            d_skip[layer_index],
        )
        gated_out = (core_out * gate_gain[layer_index][None, :]).astype(jnp.bfloat16)
        back_branch = (upstream * factor).astype(jnp.bfloat16)
        grad_wout = weight_grad(back_branch, gated_out)
        back_factor = jnp.sum(upstream * update, axis=1, keepdims=True)
        back_square = -0.5 * back_factor * factor * factor * factor
        back_gated = input_back(back_branch, w_out[layer_index])
        grad_gate = jnp.sum(back_gated * core_out, axis=0)
        back_core = (
            back_gated * gate_gain[layer_index][None, :] + back_square * 2.0 * core_out / INNER
        )
        (
            back_inner,
            back_state,
            back_step,
            back_gate,
            grad_kx,
            grad_sx,
            grad_kbc,
            grad_sbc,
            grad_bias,
            grad_decay,
            grad_skip,
        ) = pull(back_core)
        back_inner = back_inner.astype(jnp.bfloat16)
        back_state = back_state.astype(jnp.bfloat16)
        back_step = back_step.astype(jnp.bfloat16)
        back_gate = back_gate.astype(jnp.bfloat16)
        grad_wz = weight_grad(normed, back_gate)
        grad_wx = weight_grad(normed, back_inner)
        grad_wbc = weight_grad(normed, back_state)
        grad_wdt = weight_grad(normed, back_step)
        local_normed = (
            input_back(back_gate, w_z[layer_index])
            + input_back(back_inner, w_x[layer_index])
            + input_back(back_state, w_bc[layer_index])
            + input_back(back_step, w_dt[layer_index])
        )
        back_normed = row_sum(local_normed, "tensor", tensor_size)
        grad_norm = jnp.sum(back_normed * residual * rescale, axis=0)
        back_hat = back_normed * norm_gain[layer_index][None, :]
        upstream = (
            upstream
            + rescale * back_hat
            - rescale
            * rescale
            * rescale
            * residual
            * jnp.mean(back_hat * residual, axis=1, keepdims=True)
        )
        owned.append(
            reduce_grads(
                dp_size,
                tensor_size,
                grad_norm,
                grad_wz,
                grad_wx,
                grad_wdt,
                grad_wout,
                jnp.concatenate([grad_kx, grad_sx[None, :], grad_gate[None, :]], axis=0),
                grad_wbc,
                jnp.concatenate([grad_kbc, grad_sbc[None, :]], axis=0),
                jnp.stack([grad_decay, grad_skip, grad_bias]),
            )
        )
    stacked = tuple(jnp.stack([owned[1][item], owned[0][item]]) for item in range(9))
    return (output, upstream) + stacked


def solution(mesh):
    placed = (
        P("dp", None),
        P("dp", None),
        P(),
        P(None, None, "tensor"),
        P(None, None, "tensor"),
        P(),
        P(None, None, "tensor"),
        P(None, None, "tensor"),
        P(None, "tensor"),
        P(),
        P(),
        P(None, "tensor"),
        P(None, "tensor"),
        P(None, "tensor"),
        P(None, "tensor"),
        P(None, "tensor", None),
    )
    return jax.shard_map(
        functools.partial(on_device, mesh.shape["dp"], mesh.shape["tensor"]),
        mesh=mesh,
        in_specs=placed,
        out_specs=(
            P("dp", None),
            P("dp", None),
            P(None, "dp"),
            P(None, "dp", "tensor"),
            P(None, "dp", "tensor"),
            P(None, "dp", "tensor"),
            P(None, "tensor", "dp"),
            P(None, None, "tensor", "dp"),
            P(None, ("dp", "tensor"), None),
            P(None, None, ("dp", "tensor")),
            P(None, None, "tensor"),
        ),
        check_vma=False,
    )
```

```python
import functools

import jax
import jax.numpy as jnp
from jax import lax
from jax.experimental import pallas as pl
from jax.experimental.pallas import tpu as pltpu
from jax.sharding import PartitionSpec as P

INNER = 1536
P_SIZE = 64
K = 4
LANES = 128
LENGTH = 256
LAYERS = 2


EPSILON = 1e-05
HIGHEST_PREC = lax.Precision.HIGHEST


def matmul(left, right, dims=((1,), (0,)), precision=None):
    return lax.dot_general(
        left, right, (dims, ((), ())), precision=precision, preferred_element_type=jnp.float32
    )


ROWS_ROWS = ((0,), (0,))
COLS_COLS = ((1,), (1,))


def exact(left, right, dims=((1,), (0,))):
    return matmul(left, right, dims, HIGHEST_PREC)


def sigmoid(value):
    return 1.0 / (1.0 + jnp.exp(-value))


def softplus(value):
    return jnp.maximum(value, 0.0) + jnp.log1p(jnp.exp(-jnp.abs(value)))


def delayed(signal, shift):
    if shift == 0:
        return signal
    rows = signal.shape[0]
    moved = pltpu.roll(signal, shift % rows, 0)
    at = lax.broadcasted_iota(jnp.int32, signal.shape, 0)
    inside = at >= shift if shift > 0 else at < rows + shift
    return jnp.where(inside, moved, 0.0)


def causal_conv(signal, taps, offset):
    total = offset
    for k in range(K):
        total = total + taps[k : k + 1, :] * delayed(signal, K - 1 - k)
    return total


def conv_back(signal, taps, back):
    total = jnp.zeros_like(signal)
    tap_grads = []
    for k in range(K):
        total = total + taps[k : k + 1, :] * delayed(back, k + 1 - K)
        tap_grads.append(jnp.sum(back * delayed(signal, K - 1 - k), axis=0, keepdims=True))
    return total, tap_grads


def triangle(rows):
    down = lax.broadcasted_iota(jnp.int32, (rows, rows), 0)
    across = lax.broadcasted_iota(jnp.int32, (rows, rows), 1)
    return down >= across


def head_map(channels):
    channel = lax.broadcasted_iota(jnp.int32, (channels, LANES), 0)
    head = lax.broadcasted_iota(jnp.int32, (channels, LANES), 1)
    return jnp.where(channel // P_SIZE == head, 1.0, 0.0)


def decay_of(log_decay, log_decay_t, head, causal):
    gap = log_decay[:, head : head + 1] - log_decay_t[head : head + 1, :]
    return jnp.where(causal, jnp.exp(jnp.where(causal, gap, 0.0)), 0.0)


def forward_kernel(
    heads,
    resid,
    gain,
    wz,
    wx,
    wbc,
    wdt,
    kx,
    kbc,
    hvec,
    gate,
    wout,
    normed_o,
    zg_o,
    xi_o,
    bci_o,
    dti_o,
    y_o,
    partial_o,
    square_o,
):
    h = resid[...]
    rows = h.shape[0]
    scale = lax.rsqrt(jnp.mean(h * h, axis=1, keepdims=True) + EPSILON)
    normed = (h * scale * gain[...]).astype(jnp.bfloat16)
    normed_o[...] = normed
    zg = matmul(normed, wz[...])
    xi = matmul(normed, wx[...])
    bci = matmul(normed, wbc[...])
    dti = matmul(normed, wdt[...])
    zg_o[...] = zg
    xi_o[...] = xi
    bci_o[...] = bci
    dti_o[...] = dti
    pre_x = causal_conv(xi, kx, kx[K : K + 1, :])
    xc = pre_x * sigmoid(pre_x)
    pre_b = causal_conv(bci, kbc, kbc[K : K + 1, :])
    bcc = pre_b * sigmoid(pre_b)
    state = bcc.shape[1] // 2
    dt = softplus(dti + hvec[2:3, :])
    rate = -jnp.exp(hvec[0:1, :]) * dt
    causal = triangle(rows)
    lower = jnp.where(causal, 1.0, 0.0)
    log_decay = exact(lower, rate)
    log_decay_t = exact(rate, lower, ((0,), (1,)))
    spread = head_map(xc.shape[1])
    xdt = xc * exact(dt, spread, COLS_COLS)
    scores = exact(bcc[:, state:], bcc[:, :state], COLS_COLS)
    for head in range(heads):
        cols = slice(head * P_SIZE, (head + 1) * P_SIZE)
        weights = scores * decay_of(log_decay, log_decay_t, head, causal)
        y_o[:, cols] = exact(weights, xdt[:, cols])
    y = y_o[...] + exact(hvec[0:8, :], spread, COLS_COLS)[1:2, :] * xc
    y_o[...] = y
    core = y * (zg * sigmoid(zg))
    square_o[...] = jnp.sum(core * core, axis=1, keepdims=True)
    gated = (core * gate[...]).astype(jnp.bfloat16)
    partial_o[...] = matmul(gated, wout[...])


def backward_kernel(
    heads,
    up,
    branch,
    factor,
    normed_r,
    zg_r,
    xi_r,
    bci_r,
    dti_r,
    y_r,
    wz,
    wx,
    wbc,
    wdt,
    kx,
    kbc,
    hvec,
    gate,
    wout,
    gwz_o,
    gwx_o,
    gwout_o,
    gwbc_o,
    gwdt_o,
    gchan_o,
    gbcc_o,
    gheads_o,
    dnormed_o,
    dxdt_s,
):
    g = up[...]
    f = factor[...]
    normed = normed_r[...]
    db = (g * f).astype(jnp.bfloat16)
    zg = zg_r[...]
    y = y_r[...]
    sz = sigmoid(zg)
    silu = zg * sz
    core = y * silu
    gated = (core * gate[...]).astype(jnp.bfloat16)
    gwout_o[...] = matmul(db, gated, ROWS_ROWS)
    dgated = matmul(db, wout[...], COLS_COLS)
    dms = -0.5 * f * f * f * jnp.sum(g * branch[...], axis=1, keepdims=True)
    gchan_o[K + 1 : K + 2, :] = jnp.sum(dgated * core, axis=0, keepdims=True)
    dcore = dgated * gate[...] + dms * (2.0 / INNER) * core
    dy = dcore * silu
    dzg = (dcore * y * (sz * (1.0 + zg * (1.0 - sz)))).astype(jnp.bfloat16)
    gwz_o[...] = matmul(normed, dzg, ROWS_ROWS)
    back = matmul(dzg, wz[...], COLS_COLS)

    xi = xi_r[...]
    bci = bci_r[...]
    dti = dti_r[...]
    rows = xi.shape[0]
    pre_x = causal_conv(xi, kx, kx[K : K + 1, :])
    sx = sigmoid(pre_x)
    xc = pre_x * sx
    pre_b = causal_conv(bci, kbc, kbc[K : K + 1, :])
    sb = sigmoid(pre_b)
    bcc = pre_b * sb
    state = bcc.shape[1] // 2
    keys = bcc[:, :state]
    queries = bcc[:, state:]
    raw = dti + hvec[2:3, :]
    dt = softplus(raw)
    neg = -jnp.exp(hvec[0:1, :])
    rate = neg * dt
    causal = triangle(rows)
    lower = jnp.where(causal, 1.0, 0.0)
    log_decay = exact(lower, rate)
    log_decay_t = exact(rate, lower, ((0,), (1,)))
    spread = head_map(xc.shape[1])
    dt_full = exact(dt, spread, COLS_COLS)
    xdt = xc * dt_full
    scores = exact(queries, keys, COLS_COLS)
    skip = exact(hvec[0:8, :], spread, COLS_COLS)[1:2, :]
    dscores = jnp.zeros_like(scores)
    for head in range(heads):
        cols = slice(head * P_SIZE, (head + 1) * P_SIZE)
        decay = decay_of(log_decay, log_decay_t, head, causal)
        dy_h = dy[:, cols]
        dscores = dscores + exact(dy_h, xdt[:, cols], COLS_COLS) * decay
        dxdt_s[:, cols] = exact(scores * decay, dy_h, ROWS_ROWS)
    dxdt = dxdt_s[...]
    dlog = exact(dy * (y - skip * xc) - xdt * dxdt, spread)
    drate = exact(lower, dlog, ROWS_ROWS)
    ddt = exact(dxdt * xc, spread) + drate * neg
    draw = ddt * sigmoid(raw)
    gheads_o[0:1, :] = jnp.sum(drate * rate, axis=0, keepdims=True)
    gheads_o[1:2, :] = jnp.sum(exact(dy * xc, spread), axis=0, keepdims=True)
    gheads_o[2:3, :] = jnp.sum(draw, axis=0, keepdims=True)
    gheads_o[3:8, :] = jnp.zeros((5, LANES), jnp.float32)
    ddti = draw.astype(jnp.bfloat16)
    gwdt_o[...] = matmul(normed, ddti, ROWS_ROWS)
    back = back + matmul(ddti, wdt[...], COLS_COLS)

    dpre_x = (dxdt * dt_full + skip * dy) * (sx * (1.0 + pre_x * (1.0 - sx)))
    dxi, taps_x = conv_back(xi, kx, dpre_x)
    for k in range(K):
        gchan_o[k : k + 1, :] = taps_x[k]
    gchan_o[K : K + 1, :] = jnp.sum(dpre_x, axis=0, keepdims=True)
    dxi = dxi.astype(jnp.bfloat16)
    gwx_o[...] = matmul(normed, dxi, ROWS_ROWS)
    back = back + matmul(dxi, wx[...], COLS_COLS)

    dkeys = exact(dscores, queries, ROWS_ROWS)
    dqueries = exact(dscores, keys)
    dbcc = jnp.concatenate([dkeys, dqueries], axis=1)
    dpre_b = dbcc * (sb * (1.0 + pre_b * (1.0 - sb)))
    dbci, taps_b = conv_back(bci, kbc, dpre_b)
    for k in range(K):
        gbcc_o[k : k + 1, :] = taps_b[k]
    gbcc_o[K : K + 1, :] = jnp.sum(dpre_b, axis=0, keepdims=True)
    dbci = dbci.astype(jnp.bfloat16)
    gwbc_o[...] = matmul(normed, dbci, ROWS_ROWS)
    dnormed_o[...] = back + matmul(dbci, wbc[...], COLS_COLS)


def run_kernel(body, args, outs, scratch=()):
    return pl.pallas_call(
        body,
        out_shape=[jax.ShapeDtypeStruct(shape, dtype) for shape, dtype in outs],
        in_specs=[pl.BlockSpec(memory_space=pltpu.VMEM)] * len(args),
        out_specs=[pl.BlockSpec(memory_space=pltpu.VMEM)] * len(outs),
        scratch_shapes=list(scratch),
        compiler_params=pltpu.CompilerParams(vmem_limit_bytes=48 * 1024 * 1024),
    )(*args)


def exchange(value, axis, size, bit):
    step = 1 << bit
    return lax.ppermute(value, axis, [(i, i ^ step) for i in range(size)])


def bit_of(axis, bit):
    return (lax.axis_index(axis) >> bit) & 1


def halve(value, axis, size, bit, dim):
    mine = bit_of(axis, bit)
    keep = lax.dynamic_index_in_dim(value, mine, dim, keepdims=False)
    send = lax.dynamic_index_in_dim(value, 1 - mine, dim, keepdims=False)
    return keep + exchange(send, axis, size, bit)


def scatter_sum(value, axis, size, dim):
    left = size
    bit = 0
    while left > 1:
        left //= 2
        shape = value.shape
        value = value.reshape(shape[:dim] + (left, 2) + shape[dim + 1 :])
        value = halve(value, axis, size, bit, dim + 1)
        bit += 1
    return lax.squeeze(value, (dim,))


def full_sum(value, axis, size, first=0):
    bit = first
    while (1 << bit) < size:
        value = value + exchange(value, axis, size, bit)
        bit += 1
    return value


def row_sum(value, axis, size, chunks=2):
    rows, width = value.shape
    mine = bit_of(axis, 0)
    parts = value.reshape(chunks, 2, rows // (2 * chunks), width)
    done = []
    for index in range(chunks):
        half = halve(parts[index], axis, size, 0, 0)
        half = full_sum(half, axis, size, 1)
        other = exchange(half, axis, size, 0)
        low = jnp.where(mine == 0, half, other)
        high = jnp.where(mine == 0, other, half)
        done += [low, high]
    return jnp.concatenate(done, axis=0)


def reduce_grads(dp_size, tensor_size, g_norm, g_wz, g_wx, g_wdt, g_wout, g_chan, g_wbc, g_bcc, g_heads):
    width = g_norm.shape[0]
    own = width // dp_size
    heads = g_wdt.shape[1]
    channels = g_wz.shape[1]
    taps = g_chan.shape[0]
    lanes = P_SIZE // dp_size

    def blocks(grad):
        return grad.reshape(dp_size, own, channels)

    out_t = scatter_sum(blocks(g_wout), "dp", dp_size, 0)
    r_wx = scatter_sum(blocks(g_wx), "dp", dp_size, 0)
    r_wz = scatter_sum(blocks(g_wz), "dp", dp_size, 0)
    chan = g_chan.reshape(taps, heads, dp_size, lanes).transpose(2, 0, 1, 3)
    small = jnp.concatenate(
        [
            g_wdt.reshape(dp_size, own * heads),
            g_norm.reshape(dp_size, own),
            chan.reshape(dp_size, taps * heads * lanes),
            jnp.broadcast_to(g_heads.reshape(1, 3 * heads), (dp_size, 3 * heads)),
        ],
        axis=1,
    )
    used = small.shape[1]
    padded = -(-used // 1024) * 1024
    small = jnp.pad(small, ((0, 0), (0, padded - used))).reshape(dp_size, padded // 128, 128)
    small = scatter_sum(small, "dp", dp_size, 0).reshape(padded)
    at = [own * heads, own, taps * heads * lanes, 3 * heads]
    r_wdt = small[: at[0]].reshape(own, heads)
    r_norm = small[at[0] : at[0] + at[1]]
    r_chan = small[at[0] + at[1] : sum(at[:3])].reshape(taps, heads, lanes)
    r_heads = small[sum(at[:3]) : used].reshape(3, heads)
    both = g_wbc.shape[1]
    cut = width // (dp_size * tensor_size)
    piece = both // (dp_size * tensor_size)
    rows = g_bcc.shape[0]
    conv = g_bcc.reshape(rows, dp_size, tensor_size, piece).transpose(1, 2, 0, 3)
    conv = conv.reshape(dp_size, tensor_size, 1, rows * piece)
    conv = jnp.pad(conv, ((0, 0), (0, 0), (0, 0), (0, both - rows * piece)))
    shared = jnp.concatenate([g_wbc.reshape(dp_size, tensor_size, cut, both), conv], axis=2)
    shared = scatter_sum(shared, "tensor", tensor_size, 1)
    shared = scatter_sum(shared, "dp", dp_size, 0)
    r_wbc = shared[:cut]
    r_bcc = shared[cut, : rows * piece].reshape(rows, piece)
    return (r_norm, r_wz, r_wx, r_wdt, out_t.T, r_chan, r_wbc, r_bcc, r_heads)


def on_device(
    dp_size,
    tensor_size,
    tokens,
    cotangent,
    norm_gain,
    w_z,
    w_x,
    w_bc,
    w_dt,
    conv_x,
    conv_x_bias,
    conv_bc,
    conv_bc_bias,
    dt_bias,
    a_log,
    d_skip,
    gate_gain,
    w_out,
):
    rows, width = tokens.shape
    assert rows == LENGTH
    heads = w_dt.shape[2]
    channels = w_z.shape[2]
    both = w_bc.shape[2]
    f32, bf16 = jnp.float32, jnp.bfloat16
    spare = LANES - heads
    w_dt = jnp.pad(w_dt, ((0, 0), (0, 0), (0, spare)))
    hvecs = jnp.pad(jnp.stack([a_log, d_skip, dt_bias], axis=1), ((0, 0), (0, 5), (0, spare)))
    taps_x = jnp.concatenate([conv_x, conv_x_bias[:, None, :]], axis=1)
    taps_b = jnp.concatenate([conv_bc, conv_bc_bias[:, None, :]], axis=1)
    residual = tokens.astype(f32)
    saved = []
    for layer in range(LAYERS):
        weights = (
            w_z[layer],
            w_x[layer],
            w_bc[layer],
            w_dt[layer],
            taps_x[layer],
            taps_b[layer],
            hvecs[layer],
            gate_gain[layer][None, :],
            w_out[layer],
        )
        *kept, partial, square = run_kernel(
            functools.partial(forward_kernel, heads),
            (residual, norm_gain[layer][None, :]) + weights,
            (
                ((rows, width), bf16),
                ((rows, channels), f32),
                ((rows, channels), f32),
                ((rows, both), f32),
                ((rows, LANES), f32),
                ((rows, channels), f32),
                ((rows, width), f32),
                ((rows, 1), f32),
            ),
        )
        total_square = full_sum(square.reshape(rows // 128, 128), "tensor", tensor_size)
        factor = lax.rsqrt(total_square.reshape(rows, 1) / INNER + EPSILON)
        branch = row_sum(partial, "tensor", tensor_size)
        saved.append((residual, kept, weights, branch, factor))
        residual = residual + factor * branch
    output = residual
    upstream = cotangent.astype(f32)
    owned = []
    for layer in reversed(range(LAYERS)):
        residual, kept, weights, branch, factor = saved[layer]
        gwz, gwx, gwout, gwbc, gwdt, gchan, gbcc, gheads, local_normed = run_kernel(
            functools.partial(backward_kernel, heads),
            (upstream, branch, factor) + tuple(kept) + weights,
            (
                ((width, channels), f32),
                ((width, channels), f32),
                ((width, channels), f32),
                ((width, both), f32),
                ((width, LANES), f32),
                ((K + 2, channels), f32),
                ((K + 1, both), f32),
                ((8, LANES), f32),
                ((rows, width), f32),
            ),
            (pltpu.VMEM((rows, channels), f32),),
        )
        back_normed = row_sum(local_normed, "tensor", tensor_size)
        rescale = lax.rsqrt(jnp.mean(residual * residual, axis=1, keepdims=True) + EPSILON)
        grad_norm = jnp.sum(back_normed * residual * rescale, axis=0)
        back_hat = back_normed * norm_gain[layer][None, :]
        upstream = (
            upstream
            + rescale * back_hat
            - rescale
            * rescale
            * rescale
            * residual
            * jnp.mean(back_hat * residual, axis=1, keepdims=True)
        )
        owned.append(
            reduce_grads(
                dp_size,
                tensor_size,
                grad_norm,
                gwz,
                gwx,
                gwdt[:, :heads],
                gwout,
                gchan,
                gwbc,
                gbcc,
                gheads[:3, :heads],
            )
        )
    stacked = tuple(jnp.stack([owned[1][item], owned[0][item]]) for item in range(9))
    return (output, upstream) + stacked


def solution(mesh):
    placed = (
        P("dp", None),
        P("dp", None),
        P(),
        P(None, None, "tensor"),
        P(None, None, "tensor"),
        P(),
        P(None, None, "tensor"),
        P(None, None, "tensor"),
        P(None, "tensor"),
        P(),
        P(),
        P(None, "tensor"),
        P(None, "tensor"),
        P(None, "tensor"),
        P(None, "tensor"),
        P(None, "tensor", None),
    )
    return jax.shard_map(
        functools.partial(on_device, mesh.shape["dp"], mesh.shape["tensor"]),
        mesh=mesh,
        in_specs=placed,
        out_specs=(
            P("dp", None),
            P("dp", None),
            P(None, "dp"),
            P(None, "dp", "tensor"),
            P(None, "dp", "tensor"),
            P(None, "dp", "tensor"),
            P(None, "tensor", "dp"),
            P(None, None, "tensor", "dp"),
            P(None, ("dp", "tensor"), None),
            P(None, None, ("dp", "tensor")),
            P(None, None, "tensor"),
        ),
        check_vma=False,
    )
```

```python
import functools

import jax
import jax.numpy as jnp
from jax import lax
from jax.experimental import pallas as pl
from jax.experimental.pallas import tpu as pltpu
from jax.sharding import PartitionSpec as P

INNER = 1536
P_SIZE = 64
K = 4
LANES = 128
LENGTH = 256
LAYERS = 2


EPSILON = 1e-05
HIGHEST_PREC = lax.Precision.HIGHEST


def matmul(left, right, dims=((1,), (0,)), precision=None):
    return lax.dot_general(
        left, right, (dims, ((), ())), precision=precision, preferred_element_type=jnp.float32
    )


ROWS_ROWS = ((0,), (0,))
COLS_COLS = ((1,), (1,))


def exact(left, right, dims=((1,), (0,))):
    return matmul(left, right, dims, HIGHEST_PREC)


def sigmoid(value):
    return 1.0 / (1.0 + jnp.exp(-value))


def softplus(value):
    return jnp.maximum(value, 0.0) + jnp.log1p(jnp.exp(-jnp.abs(value)))


def delayed(signal, shift):
    if shift == 0:
        return signal
    rows = signal.shape[0]
    moved = pltpu.roll(signal, shift % rows, 0)
    at = lax.broadcasted_iota(jnp.int32, signal.shape, 0)
    inside = at >= shift if shift > 0 else at < rows + shift
    return jnp.where(inside, moved, 0.0)


def causal_conv(signal, taps, offset):
    total = offset
    for k in range(K):
        total = total + taps[k : k + 1, :] * delayed(signal, K - 1 - k)
    return total


def conv_back(signal, taps, back):
    total = jnp.zeros_like(signal)
    tap_grads = []
    for k in range(K):
        total = total + taps[k : k + 1, :] * delayed(back, k + 1 - K)
        tap_grads.append(jnp.sum(back * delayed(signal, K - 1 - k), axis=0, keepdims=True))
    return total, tap_grads


def triangle(rows):
    down = lax.broadcasted_iota(jnp.int32, (rows, rows), 0)
    across = lax.broadcasted_iota(jnp.int32, (rows, rows), 1)
    return down >= across


def head_map(channels):
    channel = lax.broadcasted_iota(jnp.int32, (channels, LANES), 0)
    head = lax.broadcasted_iota(jnp.int32, (channels, LANES), 1)
    return jnp.where(channel // P_SIZE == head, 1.0, 0.0)


def decay_of(log_decay, log_decay_t, head, causal):
    gap = log_decay[:, head : head + 1] - log_decay_t[head : head + 1, :]
    return jnp.where(causal, jnp.exp(jnp.where(causal, gap, 0.0)), 0.0)


def forward_kernel(
    heads,
    resid,
    gain,
    wz,
    wx,
    wbc,
    wdt,
    kx,
    kbc,
    hvec,
    gate,
    wout,
    normed_o,
    zg_o,
    xi_o,
    bci_o,
    dti_o,
    y_o,
    partial_o,
    square_o,
):
    h = resid[...]
    rows = h.shape[0]
    scale = lax.rsqrt(jnp.mean(h * h, axis=1, keepdims=True) + EPSILON)
    normed = (h * scale * gain[...]).astype(jnp.bfloat16)
    normed_o[...] = normed
    zg = matmul(normed, wz[...])
    xi = matmul(normed, wx[...])
    bci = matmul(normed, wbc[...])
    dti = matmul(normed, wdt[...])
    zg_o[...] = zg
    xi_o[...] = xi
    bci_o[...] = bci
    dti_o[...] = dti
    pre_x = causal_conv(xi, kx, kx[K : K + 1, :])
    xc = pre_x * sigmoid(pre_x)
    pre_b = causal_conv(bci, kbc, kbc[K : K + 1, :])
    bcc = pre_b * sigmoid(pre_b)
    state = bcc.shape[1] // 2
    dt = softplus(dti + hvec[2:3, :])
    rate = -jnp.exp(hvec[0:1, :]) * dt
    causal = triangle(rows)
    lower = jnp.where(causal, 1.0, 0.0)
    log_decay = exact(lower, rate)
    log_decay_t = exact(rate, lower, ((0,), (1,)))
    spread = head_map(xc.shape[1])
    xdt = xc * exact(dt, spread, COLS_COLS)
    scores = exact(bcc[:, state:], bcc[:, :state], COLS_COLS)
    for head in range(heads):
        cols = slice(head * P_SIZE, (head + 1) * P_SIZE)
        weights = scores * decay_of(log_decay, log_decay_t, head, causal)
        y_o[:, cols] = exact(weights, xdt[:, cols])
    y = y_o[...] + exact(hvec[0:8, :], spread, COLS_COLS)[1:2, :] * xc
    y_o[...] = y
    core = y * (zg * sigmoid(zg))
    square_o[...] = jnp.sum(core * core, axis=1, keepdims=True)
    gated = (core * gate[...]).astype(jnp.bfloat16)
    partial_o[...] = matmul(gated, wout[...])


def backward_kernel(
    heads,
    up,
    branch,
    factor,
    normed_r,
    zg_r,
    xi_r,
    bci_r,
    dti_r,
    y_r,
    wz,
    wx,
    wbc,
    wdt,
    kx,
    kbc,
    hvec,
    gate,
    wout,
    gin_o,
    gwout_o,
    gwbc_o,
    gwdt_o,
    gchan_o,
    gbcc_o,
    gheads_o,
    dnormed_o,
    dxdt_s,
):
    g = up[...]
    f = factor[...]
    normed = normed_r[...]
    db = (g * f).astype(jnp.bfloat16)
    zg = zg_r[...]
    y = y_r[...]
    sz = sigmoid(zg)
    silu = zg * sz
    core = y * silu
    gated = (core * gate[...]).astype(jnp.bfloat16)
    gwout_o[...] = matmul(db, gated, ROWS_ROWS)
    dgated = matmul(db, wout[...], COLS_COLS)
    dms = -0.5 * f * f * f * jnp.sum(g * branch[...], axis=1, keepdims=True)
    gchan_o[K + 1 : K + 2, :] = jnp.sum(dgated * core, axis=0, keepdims=True)
    dcore = dgated * gate[...] + dms * (2.0 / INNER) * core
    dy = dcore * silu
    dzg = (dcore * y * (sz * (1.0 + zg * (1.0 - sz)))).astype(jnp.bfloat16)
    channels = dzg.shape[1]
    gin_o[:, :channels] = matmul(normed, dzg, ROWS_ROWS)
    back = matmul(dzg, wz[...], COLS_COLS)

    xi = xi_r[...]
    bci = bci_r[...]
    dti = dti_r[...]
    rows = xi.shape[0]
    pre_x = causal_conv(xi, kx, kx[K : K + 1, :])
    sx = sigmoid(pre_x)
    xc = pre_x * sx
    pre_b = causal_conv(bci, kbc, kbc[K : K + 1, :])
    sb = sigmoid(pre_b)
    bcc = pre_b * sb
    state = bcc.shape[1] // 2
    keys = bcc[:, :state]
    queries = bcc[:, state:]
    raw = dti + hvec[2:3, :]
    dt = softplus(raw)
    neg = -jnp.exp(hvec[0:1, :])
    rate = neg * dt
    causal = triangle(rows)
    lower = jnp.where(causal, 1.0, 0.0)
    log_decay = exact(lower, rate)
    log_decay_t = exact(rate, lower, ((0,), (1,)))
    spread = head_map(xc.shape[1])
    dt_full = exact(dt, spread, COLS_COLS)
    xdt = xc * dt_full
    scores = exact(queries, keys, COLS_COLS)
    skip = exact(hvec[0:8, :], spread, COLS_COLS)[1:2, :]
    dscores = jnp.zeros_like(scores)
    for head in range(heads):
        cols = slice(head * P_SIZE, (head + 1) * P_SIZE)
        decay = decay_of(log_decay, log_decay_t, head, causal)
        dy_h = dy[:, cols]
        dscores = dscores + exact(dy_h, xdt[:, cols], COLS_COLS) * decay
        dxdt_s[:, cols] = exact(scores * decay, dy_h, ROWS_ROWS)
    dxdt = dxdt_s[...]
    dlog = exact(dy * (y - skip * xc) - xdt * dxdt, spread)
    drate = exact(lower, dlog, ROWS_ROWS)
    ddt = exact(dxdt * xc, spread) + drate * neg
    draw = ddt * sigmoid(raw)
    gheads_o[0:1, :] = jnp.sum(drate * rate, axis=0, keepdims=True)
    gheads_o[1:2, :] = jnp.sum(exact(dy * xc, spread), axis=0, keepdims=True)
    gheads_o[2:3, :] = jnp.sum(draw, axis=0, keepdims=True)
    gheads_o[3:8, :] = jnp.zeros((5, LANES), jnp.float32)
    ddti = draw.astype(jnp.bfloat16)
    gwdt_o[...] = matmul(normed, ddti, ROWS_ROWS)
    back = back + matmul(ddti, wdt[...], COLS_COLS)

    dpre_x = (dxdt * dt_full + skip * dy) * (sx * (1.0 + pre_x * (1.0 - sx)))
    dxi, taps_x = conv_back(xi, kx, dpre_x)
    for k in range(K):
        gchan_o[k : k + 1, :] = taps_x[k]
    gchan_o[K : K + 1, :] = jnp.sum(dpre_x, axis=0, keepdims=True)
    dxi = dxi.astype(jnp.bfloat16)
    gin_o[:, channels:] = matmul(normed, dxi, ROWS_ROWS)
    back = back + matmul(dxi, wx[...], COLS_COLS)

    dkeys = exact(dscores, queries, ROWS_ROWS)
    dqueries = exact(dscores, keys)
    dbcc = jnp.concatenate([dkeys, dqueries], axis=1)
    dpre_b = dbcc * (sb * (1.0 + pre_b * (1.0 - sb)))
    dbci, taps_b = conv_back(bci, kbc, dpre_b)
    for k in range(K):
        gbcc_o[k : k + 1, :] = taps_b[k]
    gbcc_o[K : K + 1, :] = jnp.sum(dpre_b, axis=0, keepdims=True)
    dbci = dbci.astype(jnp.bfloat16)
    gwbc_o[...] = matmul(normed, dbci, ROWS_ROWS)
    dnormed_o[...] = back + matmul(dbci, wbc[...], COLS_COLS)


def run_kernel(body, args, outs, scratch=()):
    return pl.pallas_call(
        body,
        out_shape=[jax.ShapeDtypeStruct(shape, dtype) for shape, dtype in outs],
        in_specs=[pl.BlockSpec(memory_space=pltpu.VMEM)] * len(args),
        out_specs=[pl.BlockSpec(memory_space=pltpu.VMEM)] * len(outs),
        scratch_shapes=list(scratch),
        compiler_params=pltpu.CompilerParams(vmem_limit_bytes=48 * 1024 * 1024),
    )(*args)


def exchange(value, axis, size, bit):
    step = 1 << bit
    return lax.ppermute(value, axis, [(i, i ^ step) for i in range(size)])


def bit_of(axis, bit):
    return (lax.axis_index(axis) >> bit) & 1


def halve(value, axis, size, bit, dim):
    mine = bit_of(axis, bit)
    keep = lax.dynamic_index_in_dim(value, mine, dim, keepdims=False)
    send = lax.dynamic_index_in_dim(value, 1 - mine, dim, keepdims=False)
    return keep + exchange(send, axis, size, bit)


def scatter_sum(value, axis, size, dim):
    left = size
    bit = 0
    while left > 1:
        left //= 2
        shape = value.shape
        value = value.reshape(shape[:dim] + (left, 2) + shape[dim + 1 :])
        value = halve(value, axis, size, bit, dim + 1)
        bit += 1
    return lax.squeeze(value, (dim,))


def full_sum(value, axis, size, first=0):
    bit = first
    while (1 << bit) < size:
        value = value + exchange(value, axis, size, bit)
        bit += 1
    return value


def row_sum(value, axis, size, chunks=2):
    rows, width = value.shape
    mine = bit_of(axis, 0)
    parts = value.reshape(chunks, 2, rows // (2 * chunks), width)
    done = []
    for index in range(chunks):
        half = halve(parts[index], axis, size, 0, 0)
        half = full_sum(half, axis, size, 1)
        other = exchange(half, axis, size, 0)
        low = jnp.where(mine == 0, half, other)
        high = jnp.where(mine == 0, other, half)
        done += [low, high]
    return jnp.concatenate(done, axis=0)


def reduce_grads(dp_size, tensor_size, g_norm, g_in, g_wdt, g_wout, g_chan, g_wbc, g_bcc, g_heads):
    width = g_norm.shape[0]
    own = width // dp_size
    heads = g_wdt.shape[1]
    channels = g_wout.shape[1]
    taps = g_chan.shape[0]
    lanes = P_SIZE // dp_size

    r_in = scatter_sum(g_in.reshape(dp_size, own, 2 * channels), "dp", dp_size, 0)
    out_t = scatter_sum(g_wout.reshape(dp_size, own, channels), "dp", dp_size, 0)
    r_wz, r_wx = r_in[:, :channels], r_in[:, channels:]
    chan = g_chan.reshape(taps, heads, dp_size, lanes).transpose(2, 0, 1, 3)
    small = jnp.concatenate(
        [
            g_wdt.reshape(dp_size, own * heads),
            g_norm.reshape(dp_size, own),
            chan.reshape(dp_size, taps * heads * lanes),
            jnp.broadcast_to(g_heads.reshape(1, 3 * heads), (dp_size, 3 * heads)),
        ],
        axis=1,
    )
    used = small.shape[1]
    both = g_wbc.shape[1]
    cut = width // (dp_size * tensor_size)
    padded = -(-used // both) * both
    small = jnp.pad(small, ((0, 0), (0, padded - used))).reshape(dp_size, padded // both, both)
    piece = both // (dp_size * tensor_size)
    rows = g_bcc.shape[0]
    conv = g_bcc.reshape(rows, dp_size, tensor_size, piece).transpose(1, 2, 0, 3)
    conv = conv.reshape(dp_size, tensor_size, 1, rows * piece)
    conv = jnp.pad(conv, ((0, 0), (0, 0), (0, 0), (0, both - rows * piece)))
    shared = jnp.concatenate([g_wbc.reshape(dp_size, tensor_size, cut, both), conv], axis=2)
    shared = scatter_sum(shared, "tensor", tensor_size, 1)
    shared = scatter_sum(jnp.concatenate([shared, small], axis=1), "dp", dp_size, 0)
    small = shared[cut + 1 :].reshape(padded)
    at = [own * heads, own, taps * heads * lanes, 3 * heads]
    r_wdt = small[: at[0]].reshape(own, heads)
    r_norm = small[at[0] : at[0] + at[1]]
    r_chan = small[at[0] + at[1] : sum(at[:3])].reshape(taps, heads, lanes)
    r_heads = small[sum(at[:3]) : used].reshape(3, heads)
    r_wbc = shared[:cut]
    r_bcc = shared[cut, : rows * piece].reshape(rows, piece)
    return (r_norm, r_wz, r_wx, r_wdt, out_t.T, r_chan, r_wbc, r_bcc, r_heads)


def on_device(
    dp_size,
    tensor_size,
    tokens,
    cotangent,
    norm_gain,
    w_z,
    w_x,
    w_bc,
    w_dt,
    conv_x,
    conv_x_bias,
    conv_bc,
    conv_bc_bias,
    dt_bias,
    a_log,
    d_skip,
    gate_gain,
    w_out,
):
    rows, width = tokens.shape
    assert rows == LENGTH
    heads = w_dt.shape[2]
    channels = w_z.shape[2]
    both = w_bc.shape[2]
    f32, bf16 = jnp.float32, jnp.bfloat16
    spare = LANES - heads
    w_dt = jnp.pad(w_dt, ((0, 0), (0, 0), (0, spare)))
    hvecs = jnp.pad(jnp.stack([a_log, d_skip, dt_bias], axis=1), ((0, 0), (0, 5), (0, spare)))
    taps_x = jnp.concatenate([conv_x, conv_x_bias[:, None, :]], axis=1)
    taps_b = jnp.concatenate([conv_bc, conv_bc_bias[:, None, :]], axis=1)
    residual = tokens.astype(f32)
    saved = []
    for layer in range(LAYERS):
        weights = (
            w_z[layer],
            w_x[layer],
            w_bc[layer],
            w_dt[layer],
            taps_x[layer],
            taps_b[layer],
            hvecs[layer],
            gate_gain[layer][None, :],
            w_out[layer],
        )
        *kept, partial, square = run_kernel(
            functools.partial(forward_kernel, heads),
            (residual, norm_gain[layer][None, :]) + weights,
            (
                ((rows, width), bf16),
                ((rows, channels), f32),
                ((rows, channels), f32),
                ((rows, both), f32),
                ((rows, LANES), f32),
                ((rows, channels), f32),
                ((rows, width), f32),
                ((rows, 1), f32),
            ),
        )
        total_square = full_sum(square.reshape(rows // 128, 128), "tensor", tensor_size)
        factor = lax.rsqrt(total_square.reshape(rows, 1) / INNER + EPSILON)
        branch = row_sum(partial, "tensor", tensor_size)
        saved.append((residual, kept, weights, branch, factor))
        residual = residual + factor * branch
    output = residual
    upstream = cotangent.astype(f32)
    owned = []
    for layer in reversed(range(LAYERS)):
        residual, kept, weights, branch, factor = saved[layer]
        gin, gwout, gwbc, gwdt, gchan, gbcc, gheads, local_normed = run_kernel(
            functools.partial(backward_kernel, heads),
            (upstream, branch, factor) + tuple(kept) + weights,
            (
                ((width, 2 * channels), f32),
                ((width, channels), f32),
                ((width, both), f32),
                ((width, LANES), f32),
                ((K + 2, channels), f32),
                ((K + 1, both), f32),
                ((8, LANES), f32),
                ((rows, width), f32),
            ),
            (pltpu.VMEM((rows, channels), f32),),
        )
        back_normed = row_sum(local_normed, "tensor", tensor_size)
        rescale = lax.rsqrt(jnp.mean(residual * residual, axis=1, keepdims=True) + EPSILON)
        grad_norm = jnp.sum(back_normed * residual * rescale, axis=0)
        back_hat = back_normed * norm_gain[layer][None, :]
        upstream = (
            upstream
            + rescale * back_hat
            - rescale
            * rescale
            * rescale
            * residual
            * jnp.mean(back_hat * residual, axis=1, keepdims=True)
        )
        owned.append(
            reduce_grads(
                dp_size,
                tensor_size,
                grad_norm,
                gin,
                gwdt[:, :heads],
                gwout,
                gchan,
                gwbc,
                gbcc,
                gheads[:3, :heads],
            )
        )
    stacked = tuple(jnp.stack([owned[1][item], owned[0][item]]) for item in range(9))
    return (output, upstream) + stacked


def solution(mesh):
    placed = (
        P("dp", None),
        P("dp", None),
        P(),
        P(None, None, "tensor"),
        P(None, None, "tensor"),
        P(),
        P(None, None, "tensor"),
        P(None, None, "tensor"),
        P(None, "tensor"),
        P(),
        P(),
        P(None, "tensor"),
        P(None, "tensor"),
        P(None, "tensor"),
        P(None, "tensor"),
        P(None, "tensor", None),
    )
    return jax.shard_map(
        functools.partial(on_device, mesh.shape["dp"], mesh.shape["tensor"]),
        mesh=mesh,
        in_specs=placed,
        out_specs=(
            P("dp", None),
            P("dp", None),
            P(None, "dp"),
            P(None, "dp", "tensor"),
            P(None, "dp", "tensor"),
            P(None, "dp", "tensor"),
            P(None, "tensor", "dp"),
            P(None, None, "tensor", "dp"),
            P(None, ("dp", "tensor"), None),
            P(None, None, ("dp", "tensor")),
            P(None, None, "tensor"),
        ),
        check_vma=False,
    )
```
